32 devices in a mesh: section: 8 (over y, x, core), tensor: 4 (over z).
Axes of the slice: x: 2, y: 2, z: 4, core: 2. Of those that a mesh axis runs over, the one named last changes fastest.
Arguments:
- acts: bfloat16 [8, 2, 32, 4096], P('section', None, None, 'tensor'), may hold values from -6 to 6
- grads_in: bfloat16 [8, 2, 32, 4096], P('section', None, None, 'tensor'), may hold values from -6 to 6
- head_grads: bfloat16 [8, 2, 128, 512], P('section', None, None, 'tensor'), may hold values from -6 to 6
- types: int32 [8, 2, 32], P('section'), may hold values 0 or 1
- gains: bfloat16 [8, 2, 2, 1024], P('section'), may hold values from 0.3984375 to 1.59375
- w_query: bfloat16 [8, 2, 4096, 512], P('section', None, None, 'tensor'), may hold values from -0.09375 to 0.09375
- w_key: bfloat16 [8, 2, 4096, 128], P('section', None, None, 'tensor'), may hold values from -0.09375 to 0.09375
- w_value: bfloat16 [8, 2, 4096, 128], P('section', None, None, 'tensor'), may hold values from -0.09375 to 0.09375
Outputs:
- routed: bfloat16 [8, 2, 32, 4096], P('section', None, None, 'tensor')
The draws below stay inside these ranges and needn't reach their ends.
All inputs are finite; a program needn't handle non-finite values. No bound on the sum of `types` on one device may be relied on, other than what follows from the above.
Results may differ from the reference program's by a relative error of at most 0.0055.
Values may be sent and summed in bfloat16 or wider, within the bound.
A program may use at most 64 MiB of HBM per device.

```python
import jax
import jax.numpy as jnp
from jax import lax

D = 4096
HEAD_DIM = 128
SUB = 4
SPANS = 2
TOK = 128
TOKQ = 32
N_SECTION = 8
N_TENSOR = 4


def set_ends(values, stream_key, smallest, top_value):
    longest = values.shape.index(max(values.shape))
    spots = []
    for shift in (0, 1):
        where = [jax.random.randint(jax.random.fold_in(stream_key, axis), (), 0, length) for axis, length in enumerate(values.shape)]
        where[longest] = (where[longest] + shift) % values.shape[longest]
        spots.append(tuple(where))
    return values.at[spots[0]].set(smallest).at[spots[1]].set(top_value)


def block_scale(own_key, shape, cuts, least, high):
    def one(dim, parts):
        steps = jax.random.uniform(jax.random.fold_in(jax.random.fold_in(own_key, 6), dim), (parts,), jnp.float32, least / len(cuts), high / len(cuts))
        return jnp.repeat(jnp.exp(steps), shape[dim] // parts).reshape((-1,) + (1,) * (len(shape) - dim - 1))

    gain = one(*cuts[0])
    for cut in cuts[1:]:
        gain = gain * one(*cut)
    return gain


def bell_draw(rng, dims, width, most, split=(), held_as=jnp.bfloat16):
    values = jax.random.normal(rng, dims, jnp.float32) * width
    if len(split) > 0:
        values = block_scale(rng, dims, split, -0.22, 0.18) * values
    return jnp.clip(values, min=-most, max=most).astype(held_as)


def setup_inputs(seed: int = 0) -> dict:
    keys = jax.random.split(jax.random.key(seed), 9)
    acts = bell_draw(keys[0], (N_SECTION, SPANS, TOKQ, D), 1.0, 6.0, ((0, 8), (3, 4)))
    grads_in = bell_draw(keys[1], (N_SECTION, SPANS, TOKQ, D), 1.0, 6.0, ((0, 8), (3, 4)))
    head_grads = bell_draw(keys[2], (N_SECTION, SPANS, TOK, HEAD_DIM * N_TENSOR), 1.0, 6.0, ((0, 8), (3, 4)))
    types = set_ends((jax.random.randint(keys[3], (N_SECTION, SPANS, TOKQ), 0, 2) < 1).astype(jnp.int32), jax.random.fold_in(keys[3], 1), 0, 1)
    gains = jnp.clip(1.0 + 0.12 * jax.random.normal(keys[4], (N_SECTION, SPANS, 2, D // SUB), jnp.float32), 0.3984375, 1.59375).astype(jnp.bfloat16)
    w_query = bell_draw(keys[5], (N_SECTION, SPANS, D, HEAD_DIM * N_TENSOR), D ** -0.5, 0.09375, ((0, 8), (3, 4)))
    w_key = bell_draw(keys[6], (N_SECTION, SPANS, D, HEAD_DIM), D ** -0.5, 0.09375, ((0, 8), (3, 4)))
    w_value = bell_draw(keys[7], (N_SECTION, SPANS, D, HEAD_DIM), D ** -0.5, 0.09375, ((0, 8), (3, 4)))
    return dict(acts=acts, grads_in=grads_in, head_grads=head_grads, types=types, gains=gains, w_query=w_query, w_key=w_key, w_value=w_value)


epsilon = 1e-05

def span_backward(inputs):
    x_rows, grad_rows, kind_rows, gain_pair, w_query, w_key, w_value, head_rows = inputs
    heads = w_query.shape[1] // HEAD_DIM
    groups = w_key.shape[1] // HEAD_DIM
    per_group = heads // groups
    tokens = x_rows.shape[0]
    x_float = x_rows.astype(jnp.float32)
    inverse = lax.rsqrt(lax.optimization_barrier(jnp.mean(x_float * x_float, axis=-1, keepdims=True)) + epsilon)
    gain_rows = jnp.where(kind_rows[:, None] == 1, gain_pair[1][None, :], gain_pair[0][None, :]).astype(jnp.float32)
    normed = (x_float * inverse * gain_rows).astype(jnp.bfloat16)
    queries = jnp.dot(normed, w_query, preferred_element_type=jnp.float32).astype(jnp.bfloat16).reshape(tokens, heads, HEAD_DIM)
    key_rows = jnp.dot(normed, w_key, preferred_element_type=jnp.float32).astype(jnp.bfloat16).reshape(tokens, groups, HEAD_DIM)
    value_rows = jnp.dot(normed, w_value, preferred_element_type=jnp.float32).astype(jnp.bfloat16).reshape(tokens, groups, HEAD_DIM)
    key_heads = jnp.repeat(key_rows, per_group, axis=1).astype(jnp.float32)
    value_heads = jnp.repeat(value_rows, per_group, axis=1).astype(jnp.float32)
    query_float = queries.astype(jnp.float32)
    softmax_scale = HEAD_DIM ** (-0.5)
    scores = jnp.einsum('qhd,khd->hqk', query_float, key_heads) * softmax_scale
    causal = jnp.arange(tokens)[:, None] >= jnp.arange(tokens)[None, :]
    scores = jnp.where(causal[None], scores, -1e+30)
    attn_probs = jax.nn.softmax(scores, axis=-1)
    probs_low = attn_probs.astype(jnp.bfloat16)
    out_float = head_rows.reshape(tokens, heads, HEAD_DIM).astype(jnp.float32)
    prob_grads = jnp.einsum('qhd,khd->hqk', out_float, value_heads)
    score_grads = (attn_probs * (prob_grads - lax.optimization_barrier(jnp.sum(prob_grads * attn_probs, axis=-1, keepdims=True))) * softmax_scale).astype(jnp.bfloat16)
    score_float = score_grads.astype(jnp.float32)
    query_grads = jnp.einsum('hqk,khd->qhd', score_float, key_heads).astype(jnp.bfloat16)
    key_each = jnp.einsum('hqk,qhd->khd', score_float, query_float)
    value_each = jnp.einsum('hqk,qhd->khd', probs_low.astype(jnp.float32), out_float)
    key_grads = key_each.reshape(tokens, groups, per_group, HEAD_DIM).sum(axis=2).astype(jnp.bfloat16)
    value_grads = value_each.reshape(tokens, groups, per_group, HEAD_DIM).sum(axis=2).astype(jnp.bfloat16)
    partial_value = jnp.dot(query_grads.reshape(tokens, heads * HEAD_DIM), w_query.T, preferred_element_type=jnp.float32)
    partial_value = partial_value + jnp.dot(key_grads.reshape(tokens, groups * HEAD_DIM), w_key.T, preferred_element_type=jnp.float32)
    partial_value = partial_value + jnp.dot(value_grads.reshape(tokens, groups * HEAD_DIM), w_value.T, preferred_element_type=jnp.float32)
    stat_mean = lax.optimization_barrier(jnp.mean(x_float * gain_rows * partial_value, axis=-1, keepdims=True))
    norm_grads = inverse * gain_rows * partial_value - x_float * inverse ** 3 * stat_mean
    return (grad_rows.astype(jnp.float32) + norm_grads).astype(jnp.bfloat16)

def rows_join(array):
    sections = N_SECTION // SUB
    shaped = array.reshape((sections, SUB) + array.shape[1:])
    shaped = jnp.swapaxes(shaped, 1, 2)
    return shaped.reshape((sections * SPANS, SUB * array.shape[2]) + array.shape[3:])

def cols_join(array):
    sections = N_SECTION // SUB
    shaped = array.reshape((sections, SUB) + array.shape[1:])
    shaped = jnp.moveaxis(shaped, 1, -2)
    return shaped.reshape((sections * SPANS,) + array.shape[2:-1] + (SUB * array.shape[-1],))

def reference(acts, grads_in, head_grads, types, gains, w_query, w_key, w_value):
    sections = N_SECTION // SUB
    inputs = (rows_join(acts), rows_join(grads_in), rows_join(types), cols_join(gains), cols_join(w_query), cols_join(w_key), cols_join(w_value), cols_join(head_grads))
    results = lax.map(span_backward, inputs)
    results = results.reshape(sections, SPANS, TOK, D)
    rolled = jnp.roll(results, -1, axis=0)
    rolled = rolled.at[sections - 1].set(results[0][::-1])
    shaped = rolled.reshape(sections, SPANS, SUB, TOK // SUB, D)
    shaped = jnp.swapaxes(shaped, 1, 2)
    return shaped.reshape(N_SECTION, SPANS, TOK // SUB, D)
```

```python
import jax
import jax.numpy as jnp
from jax import lax
from jax.experimental import pallas as pl
from jax.experimental.pallas import tpu as pltpu
from jax.sharding import PartitionSpec as P

SUB = 4
EPS = 1e-05
MESH = pl.DeviceIdType.MESH
F32 = jnp.float32
BF16 = jnp.bfloat16
LEFT, RIGHT, ACROSS, PAIR = 0, 1, 2, 3


def dot(a, b, dims):
    return lax.dot_general(a, b, (dims, ((), ())), preferred_element_type=F32)


def kernel(
    sections, tensors,
    acts, grads, heads, types, gains, wq, wk, wv,
    out,
    xg, kinds, gain_all, wqv, wkv, wvv, wcat, hg, gr, kindc, invc,
    kvt, dkv, dkv_in, stat, stat_z, stat_s, stat_in,
    part, part_in, xs, xr, zs0, zr0, zs1, zr1, xs1, xr1, res,
    loc, ag_s, ag_r, small_s, small_r, kv_s, kv_r, dk_s, dk_r, st_s, st_r, sp_s, sp_r,
    pair_s, pair_r, x_s, x_r, z_s, z_r, route_s, route_r,
):
    spans, rows, cols = acts.shape
    n = SUB * rows
    hd = wq.shape[2]
    kc = wk.shape[2]
    width = cols * tensors
    gcols = gains.shape[2]
    T = tensors
    t = lax.axis_index("tensor")
    sec = lax.axis_index("section")
    pos = lax.rem(sec, SUB)
    here = sec // SUB
    base = here * SUB
    xi = pos // 2
    ci = lax.rem(pos, 2)
    pos_pair = xi * 2 + (1 - ci)
    pos_x = (1 - xi) * 2 + ci
    pair_dev = (base + pos_pair, t)
    x_dev = (base + pos_x, t)
    left_dev = (sec, lax.max(t - 1, 0))
    right_dev = (sec, lax.min(t + 1, T - 1))
    before = lax.rem(here + sections - 1, sections) * SUB + pos
    after = lax.rem(here + 1, sections) * SUB + pos

    def pos_peer(k):
        return (base + lax.rem(pos + k, SUB), t)

    def z_peer(k):
        return (sec, lax.rem(t + k, T))

    def send(src, dst, ssem, rsem, dev):
        pltpu.make_async_remote_copy(
            src_ref=src, dst_ref=dst, send_sem=ssem, recv_sem=rsem, device_id=dev, device_id_type=MESH
        ).start()

    def sent(src, ssem):
        pltpu.make_async_copy(src, src, ssem).wait()

    def arrived(dst, rsem):
        pltpu.make_async_copy(dst, dst, rsem).wait()

    def rowpos(p):
        return pl.ds(pl.multiple_of(p * rows, rows), rows)

    def blk(v, p, tt):
        return xg.at[v, rowpos(p), pl.ds(pl.multiple_of(tt * cols, cols), cols)]

    own = [pltpu.make_async_copy(acts.at[v], blk(v, pos, t), loc.at[v]) for v in range(2)]
    kload = pltpu.make_async_copy(types, kinds.at[pos], loc.at[2])
    gload = pltpu.make_async_copy(gains, gain_all.at[pos], loc.at[3])
    wload = [
        pltpu.make_async_copy(wq, wqv, loc.at[4]),
        pltpu.make_async_copy(wk, wkv, loc.at[5]),
        pltpu.make_async_copy(wv, wvv, loc.at[6]),
    ]
    hload = pltpu.make_async_copy(heads, hg, loc.at[7])
    grload = pltpu.make_async_copy(grads, gr, loc.at[8])
    for copy in own + [kload, gload] + wload + [hload, grload]:
        copy.start()

    barrier = pltpu.get_barrier_semaphore()
    greeted = [pos_peer(k) for k in range(1, SUB)] + [z_peer(k) for k in range(1, T)]
    greeted += [(before, t), (after, t)]
    for dev in greeted:
        pl.semaphore_signal(barrier, inc=1, device_id=dev, device_id_type=MESH)
    pl.semaphore_wait(barrier, len(greeted))

    def ag_send(kind, v, p, tt):
        dev = (left_dev, right_dev, x_dev, pair_dev)[kind]
        send(blk(v, p, tt), blk(v, p, tt), ag_s.at[v, kind, p, tt], ag_r.at[v, p, tt], dev)

    def ag_wait(v, p, tt):
        arrived(blk(v, p, tt), ag_r.at[v, p, tt])

    def ag_sides(v, p, tt):
        @pl.when(t > 0)
        def _():
            ag_send(LEFT, v, p, tt)

        @pl.when(t < T - 1)
        def _():
            ag_send(RIGHT, v, p, tt)

    own[0].wait()
    ag_send(ACROSS, 0, pos, t)
    own[1].wait()
    ag_sides(1, pos, t)
    ag_sides(0, pos, t)
    ag_send(ACROSS, 1, pos, t)
    ag_send(PAIR, 0, pos, t)
    ag_send(PAIR, 1, pos, t)
    kload.wait()
    gload.wait()
    for k in range(1, SUB):
        send(kinds.at[pos], kinds.at[pos], small_s.at[0, k], small_r.at[0, k], pos_peer(k))
        send(gain_all.at[pos], gain_all.at[pos], small_s.at[1, k], small_r.at[1, k], pos_peer(k))

    for copy in wload:
        copy.wait()

    def join_weights(v):
        for i in range(T):
            at = pl.ds(i * cols, cols)
            wcat[v, at, :hd] = wqv[v, at, :]
            wcat[v, at, hd:] = jnp.concatenate([wkv[v, at, :], wvv[v, at, :]], axis=1)

    join_weights(0)

    ag_wait(0, pos_x, t)
    ag_sides(0, pos_x, t)
    ag_send(PAIR, 0, pos_x, t)

    for k in range(1, T):
        for low in (True, False):
            tt = t - k if low else t + k
            ok = tt >= 0 if low else tt < T
            onward = t < T - 1 if low else t > 0
            kind = RIGHT if low else LEFT

            @pl.when(ok)
            def _():
                ag_wait(1, pos, tt)

                @pl.when(onward)
                def _():
                    ag_send(kind, 1, pos, tt)

                ag_send(ACROSS, 1, pos, tt)
                ag_send(PAIR, 1, pos, tt)
                for p in (pos, pos_x):
                    ag_wait(0, p, tt)

                    @pl.when(onward)
                    def _():
                        ag_send(kind, 0, p, tt)

                    ag_send(PAIR, 0, p, tt)

        if k == 1:
            join_weights(1)
            ag_wait(1, pos_x, t)
            ag_send(PAIR, 1, pos_x, t)
    for k in range(1, T):
        for low in (True, False):
            tt = t - k if low else t + k
            ok = tt >= 0 if low else tt < T

            @pl.when(ok)
            def _():
                ag_wait(1, pos_x, tt)
                ag_send(PAIR, 1, pos_x, tt)

    for k in range(1, SUB):
        source = lax.rem(pos - k + SUB, SUB)
        arrived(kinds.at[source], small_r.at[0, k])
        arrived(gain_all.at[source], small_r.at[1, k])
    eye_r = lax.broadcasted_iota(jnp.int32, (rows, rows), 0) == lax.broadcasted_iota(
        jnp.int32, (rows, rows), 1
    )
    for v in range(2):
        for p in range(SUB):
            line = kinds[p, v : v + 1, :].astype(F32)
            column = jnp.sum(jnp.where(eye_r, line, 0.0), axis=1, keepdims=True)
            kindc[v, p * rows : (p + 1) * rows, :] = jnp.broadcast_to(column, (rows, 128))

    for v in range(2):
        for p in (pos_pair, (1 - xi) * 2 + (1 - ci)):
            for tt in range(T):
                ag_wait(v, p, tt)

    hload.wait()
    eye = lax.broadcasted_iota(jnp.int32, (n, n), 0) == lax.broadcasted_iota(jnp.int32, (n, n), 1)
    queries = []
    for v in range(2):
        speech = kindc[v, :, 0:1] > 0.5
        total = jnp.zeros((n, hd + 2 * kc), F32)
        square = jnp.zeros((n, 1), F32)
        for i in range(T):
            at = pl.ds(i * cols, cols)
            block = i * cols // gcols
            off = i * cols % gcols
            pair = gain_all[block, v, :, off : off + cols].astype(F32)
            xf = xg[v, :, at].astype(F32)
            square = square + jnp.sum(xf * xf, axis=1, keepdims=True)
            scaled = (xf * jnp.where(speech, pair[1:2, :], pair[0:1, :])).astype(BF16)
            total = total + dot(scaled, wcat[v, at, :], ((1,), (0,)))
        inverse = lax.rsqrt(square / width + EPS)
        invc[v] = jnp.broadcast_to(inverse, (n, 128))
        total = total * inverse
        queries.append(total[:, :hd].astype(BF16))
        turned = jnp.transpose(total[:, hd:]).astype(BF16)
        mine = pl.ds(pl.multiple_of(t * kc, kc), kc)
        kvt[v, 0, mine, :] = turned[:kc]
        kvt[v, 1, mine, :] = turned[kc:]
    mine = pl.ds(pl.multiple_of(t * kc, kc), kc)
    for k in range(1, T):
        send(kvt.at[:, :, mine, :], kvt.at[:, :, mine, :], kv_s.at[k], kv_r.at[k], z_peer(k))
    for k in range(1, T):
        source = lax.rem(t - k + T, T)
        theirs = kvt.at[:, :, pl.ds(pl.multiple_of(source * kc, kc), kc), :]
        arrived(theirs, kv_r.at[k])

    scale = hd ** (-0.5)
    causal = lax.broadcasted_iota(jnp.int32, (n, n), 0) >= lax.broadcasted_iota(
        jnp.int32, (n, n), 1
    )
    query_grads = []
    for v in range(2):
        kt = kvt[v, 0]
        vt = kvt[v, 1]
        og = hg[v]
        scores = dot(queries[v], kt, ((1,), (0,))) * scale
        scores = jnp.where(causal, scores, -1e30)
        top = jnp.max(scores, axis=1, keepdims=True)
        weights = jnp.exp(scores - top)
        probs = weights / jnp.sum(weights, axis=1, keepdims=True)
        pg = dot(og, vt, ((1,), (0,)))
        sg = probs * (pg - jnp.sum(pg * probs, axis=1, keepdims=True)) * scale
        sg = sg.astype(BF16)
        key_each = dot(queries[v], sg, ((0,), (0,)))
        value_each = dot(og, probs.astype(BF16), ((0,), (0,)))
        dkv[v, 0] = key_each.astype(BF16)
        dkv[v, 1] = value_each.astype(BF16)
        qg = dot(sg, kt, ((1,), (1,)))
        query_grads.append(qg.astype(BF16))
        column = jnp.sum(qg * queries[v].astype(F32), axis=1, keepdims=True)
        line = jnp.sum(jnp.where(eye, column, 0.0), axis=0, keepdims=True)
        line = line + jnp.sum(
            key_each * kt.astype(F32) + value_each * vt.astype(F32), axis=0, keepdims=True
        )
        stat[v] = jnp.broadcast_to(line, (8, n))
    for k in range(1, T):
        goal = pl.ds(pl.multiple_of(lax.rem(t + k, T) * kc, kc), kc)
        send(dkv.at[:, :, goal, :], dkv_in.at[k - 1], dk_s.at[k], dk_r.at[k], z_peer(k))
        send(stat, stat_z.at[k - 1], st_s.at[k], st_r.at[k], z_peer(k))
    summed = dkv[:, :, mine, :].astype(F32)
    for k in range(1, T):
        arrived(dkv_in.at[k - 1], dk_r.at[k])
        summed = summed + dkv_in[k - 1].astype(F32)

    for v in range(2):
        kv_rows = jnp.transpose(summed[v].reshape(2 * kc, n)).astype(BF16)
        joined = jnp.concatenate([query_grads[v], kv_rows], axis=1)
        for i in range(T):
            piece = dot(joined, wcat[v, pl.ds(i * cols, cols), :], ((1,), (1,))).astype(BF16)
            for p in range(SUB):
                part[v, p // 2, p % 2, i] = piece[p * rows : (p + 1) * rows]
            send(part.at[v, :, 1 - ci, i], part_in.at[v, :, i], pair_s.at[v, i], pair_r.at[v, i], pair_dev)

    line = stat[...]
    for k in range(1, T):
        arrived(stat_z.at[k - 1], st_r.at[k])
        line = line + stat_z[k - 1]
    stat_s[...] = line
    for k in range(1, SUB):
        send(stat_s, stat_in.at[k - 1], sp_s.at[k], sp_r.at[k], pos_peer(k))

    for i in range(T):
        arrived(part_in.at[0, :, i], pair_r.at[0, i])
        xs[i] = (part[0, 1 - xi, ci, i].astype(F32) + part_in[0, 1 - xi, i].astype(F32)).astype(BF16)
        send(xs.at[i], xr.at[i], x_s.at[i], x_r.at[i], x_dev)
    for i in range(T):
        arrived(part_in.at[1, :, i], pair_r.at[1, i])

    def held0(i):
        return (
            part[0, xi, ci, i].astype(F32) + part_in[0, xi, i].astype(F32) + xr[i].astype(F32)
        )

    def held1(i):
        return part[1, :, ci, i].astype(F32) + part_in[1, :, i].astype(F32)

    bufs = ((zs0, zr0, held0), (zs1, zr1, held1))

    def step(v, goal, right):
        stage, landing, held = bufs[v]
        side = 0 if right else 1
        first = t == 0 if right else t == T - 1
        dev = right_dev if right else left_dev

        @pl.when(first)
        def _():
            stage[goal] = held(goal).astype(BF16)

        @pl.when(jnp.logical_not(first))
        def _():
            arrived(landing.at[side, goal], z_r.at[v, side, goal])
            stage[goal] = (held(goal) + landing[side, goal].astype(F32)).astype(BF16)

        send(stage.at[goal], landing.at[side, goal], z_s.at[v, goal], z_r.at[v, side, goal], dev)

    for i in range(T - 1):
        for v in (1, 0):
            if v == 0 and i == 0:
                for j in range(T):
                    arrived(xr.at[j], x_r.at[j])
            high = T - 1 - i

            @pl.when(t < high)
            def _():
                step(v, high, True)

            @pl.when(t > i)
            def _():
                step(v, i, False)

    def settle(v):
        stage, landing, held = bufs[v]
        stage[t] = held(t).astype(BF16)

        @pl.when(t > 0)
        def _():
            arrived(landing.at[0, t], z_r.at[v, 0, t])
            stage[t] = (stage[t].astype(F32) + landing[0, t].astype(F32)).astype(BF16)

        @pl.when(t < T - 1)
        def _():
            arrived(landing.at[1, t], z_r.at[v, 1, t])
            stage[t] = (stage[t].astype(F32) + landing[1, t].astype(F32)).astype(BF16)

    settle(1)
    xs1[...] = zs1[t, 1 - xi]
    send(xs1, xr1, x_s.at[T], x_r.at[T], x_dev)
    settle(0)

    grload.wait()
    line = stat_s[...]
    for k in range(1, SUB):
        arrived(stat_in.at[k - 1], sp_r.at[k])
        line = line + stat_in[k - 1]
    lane = lax.broadcasted_iota(jnp.int32, (rows, n), 1)
    row = lax.broadcasted_iota(jnp.int32, (rows, n), 0)
    pick = lane == row + pos * rows
    gain_block = t * cols // gcols
    gain_off = pl.multiple_of(lax.rem(t * cols, gcols), cols)

    def finish(v, grad_sum):
        mean = jnp.sum(jnp.where(pick, line[v, 0:1, :], 0.0), axis=1, keepdims=True) / width
        inverse = invc[v, rowpos(pos), 0:1]
        speech = kindc[v, rowpos(pos), 0:1] > 0.5
        pair = gain_all[gain_block, v, :, pl.ds(gain_off, cols)].astype(F32)
        gain = jnp.where(speech, pair[1:2, :], pair[0:1, :])
        x = xg[v, rowpos(pos), pl.ds(pl.multiple_of(t * cols, cols), cols)].astype(F32)
        res[v] = (
            gr[v].astype(F32) + inverse * gain * grad_sum - x * (inverse * inverse * mean)
        ).astype(BF16)
        goal = jnp.where(here == 0, 1 - v, v)
        send(res.at[v], out.at[goal], route_s.at[v], route_r.at[goal], (before, t))

    finish(0, zs0[t].astype(F32))
    arrived(xr1, x_r.at[T])
    finish(1, zs1[t, xi].astype(F32) + xr1[...].astype(F32))

    for v in range(2):
        for kind in (LEFT, RIGHT):
            edge = t > 0 if kind == LEFT else t < T - 1
            for tt in range(T):
                use = jnp.logical_and(edge, tt >= t if kind == LEFT else tt <= t)
                for p in (pos, pos_x):
                    if v == 1 and p is pos_x:
                        continue

                    @pl.when(use)
                    def _():
                        sent(blk(v, p, tt), ag_s.at[v, kind, p, tt])

        for tt in range(T):
            for p in (pos, pos_x):
                sent(blk(v, p, tt), ag_s.at[v, PAIR, p, tt])
            if v == 1:
                sent(blk(v, pos, tt), ag_s.at[v, ACROSS, pos, tt])
    sent(blk(0, pos, t), ag_s.at[0, ACROSS, pos, t])
    for k in range(1, SUB):
        sent(kinds.at[pos], small_s.at[0, k])
        sent(gain_all.at[pos], small_s.at[1, k])
        sent(stat_s, sp_s.at[k])
    for k in range(1, T):
        sent(kvt.at[:, :, mine, :], kv_s.at[k])
        goal = pl.ds(pl.multiple_of(lax.rem(t + k, T) * kc, kc), kc)
        sent(dkv.at[:, :, goal, :], dk_s.at[k])
        sent(stat, st_s.at[k])
    for v in range(2):
        for i in range(T):
            sent(part.at[v, :, 1 - ci, i], pair_s.at[v, i])

            @pl.when(i != t)
            def _():
                sent(bufs[v][0].at[i], z_s.at[v, i])
    for i in range(T):
        sent(xs.at[i], x_s.at[i])
    sent(xs1, x_s.at[T])
    for v in range(2):
        sent(res.at[v], route_s.at[v])
        arrived(out.at[v], route_r.at[v])


def per_device(sections, acts, grads_in, head_grads, types, gains, w_query, w_key, w_value):
    T = lax.axis_size("tensor")
    acts, grads_in, head_grads, types, gains = acts[0], grads_in[0], head_grads[0], types[0], gains[0]
    w_query, w_key, w_value = w_query[0], w_key[0], w_value[0]
    spans, rows, cols = acts.shape
    n = SUB * rows
    hd = w_query.shape[2]
    kc = w_key.shape[2]
    width = cols * T
    V = pltpu.VMEM
    D = pltpu.SemaphoreType.DMA
    scratch = [
        V((2, n, width), BF16), V((SUB, 2, rows), jnp.int32), V((SUB,) + gains.shape, BF16),
        V(w_query.shape, BF16), V(w_key.shape, BF16), V(w_value.shape, BF16),
        V((2, width, hd + 2 * kc), BF16), V(head_grads.shape, BF16), V(grads_in.shape, BF16),
        V((2, n, 128), F32), V((2, n, 128), F32),
        V((2, 2, hd, n), BF16), V((2, 2, hd, n), BF16), V((T - 1, 2, 2, kc, n), BF16),
        V((2, 8, n), F32), V((T - 1, 2, 8, n), F32), V((2, 8, n), F32), V((SUB - 1, 2, 8, n), F32),
        V((2, 2, 2, T, rows, cols), BF16), V((2, 2, T, rows, cols), BF16),
        V((T, rows, cols), BF16), V((T, rows, cols), BF16),
        V((T, rows, cols), BF16), V((2, T, rows, cols), BF16),
        V((T, 2, rows, cols), BF16), V((2, T, 2, rows, cols), BF16),
        V((rows, cols), BF16), V((rows, cols), BF16), V((2, rows, cols), BF16),
        D((9,)), D((2, 4, SUB, T)), D((2, SUB, T)), D((2, SUB)), D((2, SUB)),
        D((T,)), D((T,)), D((T,)), D((T,)), D((T,)), D((T,)), D((SUB,)), D((SUB,)),
        D((2, T)), D((2, T)), D((T + 1,)), D((T + 1,)), D((2, T)), D((2, 2, T)), D((2,)), D((2,)),
    ]

    def body(*refs):
        kernel(sections, T, *refs)

    routed = pl.pallas_call(
        body,
        out_shape=jax.ShapeDtypeStruct((2, rows, cols), BF16),
        in_specs=[pl.BlockSpec(memory_space=pl.ANY)] * 8,
        out_specs=pl.BlockSpec(memory_space=pltpu.VMEM),
        scratch_shapes=scratch,
        compiler_params=pltpu.CompilerParams(
            collective_id=0, has_side_effects=True, vmem_limit_bytes=50 * 1024 * 1024
        ),
        name="relay",
    )(acts, grads_in, head_grads, types, gains, w_query, w_key, w_value)
    return routed[None]


def solution(mesh):
    sections = mesh.shape["section"] // SUB

    def run(*args):
        return per_device(sections, *args)

    return jax.shard_map(
        run,
        mesh=mesh,
        in_specs=(
            P("section", None, None, "tensor"),
            P("section", None, None, "tensor"),
            P("section", None, None, "tensor"),
            P("section", None, None),
            P("section", None, None, None),
            P("section", None, None, "tensor"),
            P("section", None, None, "tensor"),
            P("section", None, None, "tensor"),
        ),
        out_specs=P("section", None, None, "tensor"),
        check_vma=False,
    )
```

```python
import jax
import jax.numpy as jnp
from jax import lax
from jax.experimental import pallas as pl
from jax.experimental.pallas import tpu as pltpu
from jax.sharding import PartitionSpec as P

SUB = 4
EPS = 1e-05
MESH = pl.DeviceIdType.MESH
F32 = jnp.float32
BF16 = jnp.bfloat16
LEFT, RIGHT, ACROSS, PAIR = 0, 1, 2, 3


def dot(a, b, dims):
    return lax.dot_general(a, b, (dims, ((), ())), preferred_element_type=F32)


def kernel(
    sections, tensors,
    acts, grads, heads, types, gains, wq, wk, wv,
    out,
    xg, kinds, gain_all, wqv, wkv, wvv, wcat, hg, gr, kindc, invc, acc, square,
    kvt, dkv, dkv_in, stat, stat_z, stat_s, stat_in,
    part, part_in, xs, xr, zs0, zr0, zs1, zr1, xs1, xr1, res,
    loc, ag_s, ag_r, small_s, small_r, kv_s, kv_r, dk_s, dk_r, st_s, st_r, sp_s, sp_r,
    pair_s, pair_r, x_s, x_r, z_s, z_r, route_s, route_r,
):
    spans, rows, cols = acts.shape
    n = SUB * rows
    hd = wq.shape[2]
    kc = wk.shape[1]
    width = cols * tensors
    gcols = gains.shape[2]
    T = tensors
    t = lax.axis_index("tensor")
    sec = lax.axis_index("section")
    pos = lax.rem(sec, SUB)
    here = sec // SUB
    base = here * SUB
    xi = pos // 2
    ci = lax.rem(pos, 2)
    pos_pair = xi * 2 + (1 - ci)
    pos_x = (1 - xi) * 2 + ci
    pair_dev = (base + pos_pair, t)
    x_dev = (base + pos_x, t)
    left_dev = (sec, lax.max(t - 1, 0))
    right_dev = (sec, lax.min(t + 1, T - 1))
    before = lax.rem(here + sections - 1, sections) * SUB + pos
    after = lax.rem(here + 1, sections) * SUB + pos

    def pos_peer(k):
        return (base + lax.rem(pos + k, SUB), t)

    def z_peer(k):
        return (sec, lax.rem(t + k, T))

    def send(src, dst, ssem, rsem, dev):
        pltpu.make_async_remote_copy(
            src_ref=src, dst_ref=dst, send_sem=ssem, recv_sem=rsem, device_id=dev, device_id_type=MESH
        ).start()

    def sent(src, ssem):
        pltpu.make_async_copy(src, src, ssem).wait()

    def arrived(dst, rsem):
        pltpu.make_async_copy(dst, dst, rsem).wait()

    def rowpos(p):
        return pl.ds(pl.multiple_of(p * rows, rows), rows)

    def blk(v, p, tt):
        return xg.at[v, rowpos(p), pl.ds(pl.multiple_of(tt * cols, cols), cols)]

    own = [pltpu.make_async_copy(acts.at[v], blk(v, pos, t), loc.at[v]) for v in range(2)]
    kload = pltpu.make_async_copy(types, kinds.at[pos], loc.at[2])
    gload = pltpu.make_async_copy(gains, gain_all.at[pos], loc.at[3])
    wload = [
        pltpu.make_async_copy(wq, wqv, loc.at[4]),
        pltpu.make_async_copy(wk, wkv, loc.at[5]),
        pltpu.make_async_copy(wv, wvv, loc.at[6]),
    ]
    hload = pltpu.make_async_copy(heads, hg, loc.at[7])
    grload = pltpu.make_async_copy(grads, gr, loc.at[8])
    for copy in own + [kload, gload] + wload + [hload, grload]:
        copy.start()

    barrier = pltpu.get_barrier_semaphore()
    greeted = [pos_peer(k) for k in range(1, SUB)] + [z_peer(k) for k in range(1, T)]
    greeted += [(before, t), (after, t)]
    for dev in greeted:
        pl.semaphore_signal(barrier, inc=1, device_id=dev, device_id_type=MESH)
    pl.semaphore_wait(barrier, len(greeted))

    def ag_send(kind, v, p, tt):
        dev = (left_dev, right_dev, x_dev, pair_dev)[kind]
        send(blk(v, p, tt), blk(v, p, tt), ag_s.at[v, kind, p, tt], ag_r.at[v, p, tt], dev)

    def ag_wait(v, p, tt):
        arrived(blk(v, p, tt), ag_r.at[v, p, tt])

    def ag_sides(v, p, tt):
        @pl.when(t > 0)
        def _():
            ag_send(LEFT, v, p, tt)

        @pl.when(t < T - 1)
        def _():
            ag_send(RIGHT, v, p, tt)

    own[0].wait()
    ag_send(ACROSS, 0, pos, t)
    own[1].wait()
    ag_sides(1, pos, t)
    ag_sides(0, pos, t)
    ag_send(ACROSS, 1, pos, t)
    ag_send(PAIR, 0, pos, t)
    ag_send(PAIR, 1, pos, t)
    kload.wait()
    gload.wait()
    for k in range(1, SUB):
        send(kinds.at[pos], kinds.at[pos], small_s.at[0, k], small_r.at[0, k], pos_peer(k))
        send(gain_all.at[pos], gain_all.at[pos], small_s.at[1, k], small_r.at[1, k], pos_peer(k))

    for copy in wload:
        copy.wait()

    def join_weights(v):
        for i in range(T):
            at = pl.ds(i * cols, cols)
            wcat[v, at, :hd] = wqv[v, at, :]
            kv_cols = jnp.concatenate([wkv[v, :, at], wvv[v, :, at]], axis=0)
            wcat[v, at, hd:] = jnp.transpose(kv_cols)

    acc[...] = jnp.zeros_like(acc)
    square[...] = jnp.zeros_like(square)

    def project(tt):
        for p in (pos_pair, (1 - xi) * 2 + (1 - ci)):
            for v in range(2):
                ag_wait(v, p, tt)
        block = tt * cols // gcols
        off = pl.multiple_of(lax.rem(tt * cols, gcols), cols)
        at = pl.ds(pl.multiple_of(tt * cols, cols), cols)
        for v in range(2):
            speech = kindc[v, :, 0:1] > 0.5
            pair = gain_all[block, v, :, pl.ds(off, cols)].astype(F32)
            xf = xg[v, :, at].astype(F32)
            square[v] += jnp.broadcast_to(jnp.sum(xf * xf, axis=1, keepdims=True), (n, 128))
            scaled = (xf * jnp.where(speech, pair[1:2, :], pair[0:1, :])).astype(BF16)
            acc[v] += dot(scaled, wcat[v, at, :], ((1,), (0,)))

    join_weights(0)

    ag_wait(0, pos_x, t)
    ag_sides(0, pos_x, t)
    ag_send(PAIR, 0, pos_x, t)

    def each_side(k, action):
        for low in (True, False):
            tt = t - k if low else t + k

            @pl.when(tt >= 0 if low else tt < T)
            def _():
                action(tt, low)

    def forward(tt, low):
        onward = t < T - 1 if low else t > 0
        kind = RIGHT if low else LEFT
        ag_wait(1, pos, tt)

        @pl.when(onward)
        def _():
            ag_send(kind, 1, pos, tt)

        ag_send(ACROSS, 1, pos, tt)
        ag_send(PAIR, 1, pos, tt)
        for p in (pos, pos_x):
            ag_wait(0, p, tt)

            @pl.when(onward)
            def _():
                ag_send(kind, 0, p, tt)

            ag_send(PAIR, 0, p, tt)

    def share(tt):
        ag_wait(1, pos_x, tt)
        ag_send(PAIR, 1, pos_x, tt)

    eye_r = lax.broadcasted_iota(jnp.int32, (rows, rows), 0) == lax.broadcasted_iota(
        jnp.int32, (rows, rows), 1
    )
    for k in range(1, T):
        each_side(k, forward)
        if k == 1:
            share(t)
            join_weights(1)
            for j in range(1, SUB):
                source = lax.rem(pos - j + SUB, SUB)
                arrived(kinds.at[source], small_r.at[0, j])
                arrived(gain_all.at[source], small_r.at[1, j])
            for v in range(2):
                for p in range(SUB):
                    line = kinds[p, v : v + 1, :].astype(F32)
                    column = jnp.sum(jnp.where(eye_r, line, 0.0), axis=1, keepdims=True)
                    kindc[v, p * rows : (p + 1) * rows, :] = jnp.broadcast_to(column, (rows, 128))
            project(t)
        else:
            each_side(k - 1, lambda tt, low: share(tt))
            each_side(k - 1, lambda tt, low: project(tt))
    each_side(T - 1, lambda tt, low: share(tt))
    each_side(T - 1, lambda tt, low: project(tt))

    hload.wait()
    eye = lax.broadcasted_iota(jnp.int32, (n, n), 0) == lax.broadcasted_iota(jnp.int32, (n, n), 1)
    mine = pl.ds(pl.multiple_of(t * kc, kc), kc)
    order = (1, 0)
    queries = [None, None]
    for v in order:
        inverse = lax.rsqrt(square[v][:, 0:1] / width + EPS)
        invc[v] = jnp.broadcast_to(inverse, (n, 128))
        total = acc[v] * inverse
        turned = jnp.transpose(total[:, hd:]).astype(BF16)
        kvt[v, 0, mine, :] = turned[:kc]
        kvt[v, 1, mine, :] = turned[kc:]
        for k in range(1, T):
            block = kvt.at[v, :, mine, :]
            send(block, block, kv_s.at[v, k], kv_r.at[v, k], z_peer(k))
        queries[v] = total[:, :hd].astype(BF16)

    scale = hd ** (-0.5)
    causal = lax.broadcasted_iota(jnp.int32, (n, n), 0) >= lax.broadcasted_iota(
        jnp.int32, (n, n), 1
    )
    query_grads = [None, None]
    for v in order:
        for k in range(1, T):
            source = lax.rem(t - k + T, T)
            theirs = kvt.at[v, :, pl.ds(pl.multiple_of(source * kc, kc), kc), :]
            arrived(theirs, kv_r.at[v, k])
        kt = kvt[v, 0]
        vt = kvt[v, 1]
        og = hg[v]
        scores = dot(queries[v], kt, ((1,), (0,))) * scale
        scores = jnp.where(causal, scores, -1e30)
        top = jnp.max(scores, axis=1, keepdims=True)
        weights = jnp.exp(scores - top)
        probs = weights / jnp.sum(weights, axis=1, keepdims=True)
        pg = dot(og, vt, ((1,), (0,)))
        sg = probs * (pg - jnp.sum(pg * probs, axis=1, keepdims=True)) * scale
        sg = sg.astype(BF16)
        key_each = dot(queries[v], sg, ((0,), (0,)))
        value_each = dot(og, probs.astype(BF16), ((0,), (0,)))
        dkv[v, 0] = key_each.astype(BF16)
        dkv[v, 1] = value_each.astype(BF16)
        for k in range(1, T):
            goal = pl.ds(pl.multiple_of(lax.rem(t + k, T) * kc, kc), kc)
            send(dkv.at[v, :, goal, :], dkv_in.at[k - 1, v], dk_s.at[v, k], dk_r.at[v, k], z_peer(k))
        qg = dot(sg, kt, ((1,), (1,)))
        query_grads[v] = qg.astype(BF16)
        column = jnp.sum(qg * queries[v].astype(F32), axis=1, keepdims=True)
        line = jnp.sum(jnp.where(eye, column, 0.0), axis=0, keepdims=True)
        line = line + jnp.sum(
            key_each * kt.astype(F32) + value_each * vt.astype(F32), axis=0, keepdims=True
        )
        stat[v] = jnp.broadcast_to(line, (8, n))
    for k in range(1, T):
        send(stat, stat_z.at[k - 1], st_s.at[k], st_r.at[k], z_peer(k))

    goals = []
    for i in range((T + 1) // 2):
        goals += [T - 1 - i, i]
    goals = goals[:T]

    def terms(v, after_piece):
        summed = dkv[v, :, mine, :].astype(F32)
        for k in range(1, T):
            arrived(dkv_in.at[k - 1, v], dk_r.at[v, k])
            summed = summed + dkv_in[k - 1, v].astype(F32)
        kv_rows = jnp.transpose(summed.reshape(2 * kc, n)).astype(BF16)
        joined = jnp.concatenate([query_grads[v], kv_rows], axis=1)
        for j, i in enumerate(goals):
            piece = dot(joined, wcat[v, pl.ds(i * cols, cols), :], ((1,), (1,))).astype(BF16)
            for p in range(SUB):
                part[v, p // 2, p % 2, i] = piece[p * rows : (p + 1) * rows]
            send(part.at[v, :, 1 - ci, i], part_in.at[v, :, i], pair_s.at[v, i], pair_r.at[v, i], pair_dev)
            if j > 0:
                after_piece(goals[j - 1])
        after_piece(goals[-1])

    def held0(i):
        return (
            part[0, xi, ci, i].astype(F32) + part_in[0, xi, i].astype(F32) + xr[i].astype(F32)
        )

    def held1(i):
        return part[1, :, ci, i].astype(F32) + part_in[1, :, i].astype(F32)

    bufs = ((zs0, zr0, held0), (zs1, zr1, held1))

    def pass_on(v, goal, right):
        stage, landing, held = bufs[v]
        side = 0 if right else 1
        dev = right_dev if right else left_dev
        send(stage.at[goal], landing.at[side, goal], z_s.at[v, goal], z_r.at[v, side, goal], dev)

    def begin(v, goal):
        stage, landing, held = bufs[v]

        @pl.when(jnp.logical_and(t == 0, goal > 0))
        def _():
            stage[goal] = held(goal).astype(BF16)
            pass_on(v, goal, True)

        @pl.when(jnp.logical_and(t == T - 1, goal < T - 1))
        def _():
            stage[goal] = held(goal).astype(BF16)
            pass_on(v, goal, False)

    def relay(v, goal, right):
        stage, landing, held = bufs[v]
        side = 0 if right else 1
        arrived(landing.at[side, goal], z_r.at[v, side, goal])
        stage[goal] = (held(goal) + landing[side, goal].astype(F32)).astype(BF16)
        pass_on(v, goal, right)

    def after_one(i):
        arrived(part_in.at[1, :, i], pair_r.at[1, i])
        begin(1, i)

    def after_zero(i):
        arrived(part_in.at[0, :, i], pair_r.at[0, i])
        xs[i] = (part[0, 1 - xi, ci, i].astype(F32) + part_in[0, 1 - xi, i].astype(F32)).astype(BF16)
        send(xs.at[i], xr.at[i], x_s.at[i], x_r.at[i], x_dev)

    terms(1, after_one)

    line = stat[...]
    for k in range(1, T):
        arrived(stat_z.at[k - 1], st_r.at[k])
        line = line + stat_z[k - 1]
    stat_s[...] = line
    for k in range(1, SUB):
        send(stat_s, stat_in.at[k - 1], sp_s.at[k], sp_r.at[k], pos_peer(k))

    terms(0, after_zero)

    def relays(v, i):
        high = T - 1 - i

        @pl.when(jnp.logical_and(t > 0, t < high))
        def _():
            relay(v, high, True)

        @pl.when(jnp.logical_and(t < T - 1, t > i))
        def _():
            relay(v, i, False)

    for i in range(T - 1):
        relays(1, i)
        if i == 0:
            for goal in goals:
                arrived(xr.at[goal], x_r.at[goal])
                begin(0, goal)
        relays(0, i)

    def settle(v):
        stage, landing, held = bufs[v]
        stage[t] = held(t).astype(BF16)

        @pl.when(t > 0)
        def _():
            arrived(landing.at[0, t], z_r.at[v, 0, t])
            stage[t] = (stage[t].astype(F32) + landing[0, t].astype(F32)).astype(BF16)

        @pl.when(t < T - 1)
        def _():
            arrived(landing.at[1, t], z_r.at[v, 1, t])
            stage[t] = (stage[t].astype(F32) + landing[1, t].astype(F32)).astype(BF16)

    settle(1)
    xs1[...] = zs1[t, 1 - xi]
    send(xs1, xr1, x_s.at[T], x_r.at[T], x_dev)
    settle(0)

    grload.wait()
    line = stat_s[...]
    for k in range(1, SUB):
        arrived(stat_in.at[k - 1], sp_r.at[k])
        line = line + stat_in[k - 1]
    lane = lax.broadcasted_iota(jnp.int32, (rows, n), 1)
    row = lax.broadcasted_iota(jnp.int32, (rows, n), 0)
    pick = lane == row + pos * rows
    gain_block = t * cols // gcols
    gain_off = pl.multiple_of(lax.rem(t * cols, gcols), cols)

    def finish(v, grad_sum):
        mean = jnp.sum(jnp.where(pick, line[v, 0:1, :], 0.0), axis=1, keepdims=True) / width
        inverse = invc[v, rowpos(pos), 0:1]
        speech = kindc[v, rowpos(pos), 0:1] > 0.5
        pair = gain_all[gain_block, v, :, pl.ds(gain_off, cols)].astype(F32)
        gain = jnp.where(speech, pair[1:2, :], pair[0:1, :])
        x = xg[v, rowpos(pos), pl.ds(pl.multiple_of(t * cols, cols), cols)].astype(F32)
        res[v] = (
            gr[v].astype(F32) + inverse * gain * grad_sum - x * (inverse * inverse * mean)
        ).astype(BF16)
        goal = jnp.where(here == 0, 1 - v, v)
        send(res.at[v], out.at[goal], route_s.at[v], route_r.at[goal], (before, t))

    finish(0, zs0[t].astype(F32))
    arrived(xr1, x_r.at[T])
    finish(1, zs1[t, xi].astype(F32) + xr1[...].astype(F32))

    for v in range(2):
        for kind in (LEFT, RIGHT):
            edge = t > 0 if kind == LEFT else t < T - 1
            for tt in range(T):
                use = jnp.logical_and(edge, tt >= t if kind == LEFT else tt <= t)
                for p in (pos, pos_x):
                    if v == 1 and p is pos_x:
                        continue

                    @pl.when(use)
                    def _():
                        sent(blk(v, p, tt), ag_s.at[v, kind, p, tt])

        for tt in range(T):
            for p in (pos, pos_x):
                sent(blk(v, p, tt), ag_s.at[v, PAIR, p, tt])
            if v == 1:
                sent(blk(v, pos, tt), ag_s.at[v, ACROSS, pos, tt])
    sent(blk(0, pos, t), ag_s.at[0, ACROSS, pos, t])
    for k in range(1, SUB):
        sent(kinds.at[pos], small_s.at[0, k])
        sent(gain_all.at[pos], small_s.at[1, k])
        sent(stat_s, sp_s.at[k])
    for k in range(1, T):
        goal = pl.ds(pl.multiple_of(lax.rem(t + k, T) * kc, kc), kc)
        for v in range(2):
            sent(kvt.at[v, :, mine, :], kv_s.at[v, k])
            sent(dkv.at[v, :, goal, :], dk_s.at[v, k])
        sent(stat, st_s.at[k])
    for v in range(2):
        for i in range(T):
            sent(part.at[v, :, 1 - ci, i], pair_s.at[v, i])

            @pl.when(i != t)
            def _():
                sent(bufs[v][0].at[i], z_s.at[v, i])
    for i in range(T):
        sent(xs.at[i], x_s.at[i])
    sent(xs1, x_s.at[T])
    for v in range(2):
        sent(res.at[v], route_s.at[v])
        arrived(out.at[v], route_r.at[v])


def per_device(sections, acts, grads_in, head_grads, types, gains, w_query, w_key, w_value):
    T = lax.axis_size("tensor")
    acts, grads_in, head_grads, types, gains = acts[0], grads_in[0], head_grads[0], types[0], gains[0]
    w_query, w_key, w_value = w_query[0], jnp.swapaxes(w_key[0], 1, 2), jnp.swapaxes(w_value[0], 1, 2)
    spans, rows, cols = acts.shape
    n = SUB * rows
    hd = w_query.shape[2]
    kc = w_key.shape[1]
    width = cols * T
    V = pltpu.VMEM
    D = pltpu.SemaphoreType.DMA
    scratch = [
        V((2, n, width), BF16), V((SUB, 2, rows), jnp.int32), V((SUB,) + gains.shape, BF16),
        V(w_query.shape, BF16), V(w_key.shape, BF16), V(w_value.shape, BF16),
        V((2, width, hd + 2 * kc), BF16), V(head_grads.shape, BF16), V(grads_in.shape, BF16),
        V((2, n, 128), F32), V((2, n, 128), F32), V((2, n, hd + 2 * kc), F32), V((2, n, 128), F32),
        V((2, 2, hd, n), BF16), V((2, 2, hd, n), BF16), V((T - 1, 2, 2, kc, n), BF16),
        V((2, 8, n), F32), V((T - 1, 2, 8, n), F32), V((2, 8, n), F32), V((SUB - 1, 2, 8, n), F32),
        V((2, 2, 2, T, rows, cols), BF16), V((2, 2, T, rows, cols), BF16),
        V((T, rows, cols), BF16), V((T, rows, cols), BF16),
        V((T, rows, cols), BF16), V((2, T, rows, cols), BF16),
        V((T, 2, rows, cols), BF16), V((2, T, 2, rows, cols), BF16),
        V((rows, cols), BF16), V((rows, cols), BF16), V((2, rows, cols), BF16),
        D((9,)), D((2, 4, SUB, T)), D((2, SUB, T)), D((2, SUB)), D((2, SUB)),
        D((2, T)), D((2, T)), D((2, T)), D((2, T)), D((T,)), D((T,)), D((SUB,)), D((SUB,)),
        D((2, T)), D((2, T)), D((T + 1,)), D((T + 1,)), D((2, T)), D((2, 2, T)), D((2,)), D((2,)),
    ]

    def body(*refs):
        kernel(sections, T, *refs)

    routed = pl.pallas_call(
        body,
        out_shape=jax.ShapeDtypeStruct((2, rows, cols), BF16),
        in_specs=[pl.BlockSpec(memory_space=pl.ANY)] * 8,
        out_specs=pl.BlockSpec(memory_space=pltpu.VMEM),
        scratch_shapes=scratch,
        compiler_params=pltpu.CompilerParams(
            collective_id=0, has_side_effects=True, vmem_limit_bytes=50 * 1024 * 1024
        ),
        name="relay",
    )(acts, grads_in, head_grads, types, gains, w_query, w_key, w_value)
    return routed[None]


def solution(mesh):
    sections = mesh.shape["section"] // SUB

    def run(*args):
        return per_device(sections, *args)

    return jax.shard_map(
        run,
        mesh=mesh,
        in_specs=(
            P("section", None, None, "tensor"),
            P("section", None, None, "tensor"),
            P("section", None, None, "tensor"),
            P("section", None, None),
            P("section", None, None, None),
            P("section", None, None, "tensor"),
            P("section", None, None, "tensor"),
            P("section", None, None, "tensor"),
        ),
        out_specs=P("section", None, None, "tensor"),
        check_vma=False,
    )
```

```python
import jax
import jax.numpy as jnp
from jax import lax
from jax.experimental import pallas as pl
from jax.experimental.pallas import tpu as pltpu
from jax.sharding import PartitionSpec as P

SUB = 4
EPS = 1e-05
MESH = pl.DeviceIdType.MESH
F32 = jnp.float32
BF16 = jnp.bfloat16
LEFT, RIGHT, ACROSS, PAIR = 0, 1, 2, 3


def dot(a, b, dims):
    return lax.dot_general(a, b, (dims, ((), ())), preferred_element_type=F32)


def kernel(
    sections, tensors,
    acts, grads, heads, types, gains, wq, wk, wv,
    out,
    xg, kinds, gain_all, wqv, wkv, wvv, wcat, hg, gr, kindc, invc, acc, square,
    kvt, dkv, dkv_in, stat, stat_z, stat_s, stat_in,
    part, part_in, xs, xr, zs, zr, total, res,
    loc, ag_s, ag_r, small_s, small_r, kv_s, kv_r, dk_s, dk_r, st_s, st_r, sp_s, sp_r,
    pair_s, pair_r, x_s, x_r, z_s, z_r, route_s, route_r,
):
    spans, rows, cols = acts.shape
    n = SUB * rows
    hd = wq.shape[2]
    kc = wk.shape[1]
    width = cols * tensors
    gcols = gains.shape[2]
    T = tensors
    t = lax.axis_index("tensor")
    sec = lax.axis_index("section")
    pos = lax.rem(sec, SUB)
    here = sec // SUB
    base = here * SUB
    xi = pos // 2
    ci = lax.rem(pos, 2)
    pos_pair = xi * 2 + (1 - ci)
    pos_x = (1 - xi) * 2 + ci
    pair_dev = (base + pos_pair, t)
    x_dev = (base + pos_x, t)
    left_dev = (sec, lax.max(t - 1, 0))
    right_dev = (sec, lax.min(t + 1, T - 1))
    before = lax.rem(here + sections - 1, sections) * SUB + pos
    after = lax.rem(here + 1, sections) * SUB + pos

    def pos_peer(k):
        return (base + lax.rem(pos + k, SUB), t)

    def z_peer(k):
        return (sec, lax.rem(t + k, T))

    def send(src, dst, ssem, rsem, dev):
        pltpu.make_async_remote_copy(
            src_ref=src, dst_ref=dst, send_sem=ssem, recv_sem=rsem, device_id=dev, device_id_type=MESH
        ).start()

    def sent(src, ssem):
        pltpu.make_async_copy(src, src, ssem).wait()

    def arrived(dst, rsem):
        pltpu.make_async_copy(dst, dst, rsem).wait()

    def rowpos(p):
        return pl.ds(pl.multiple_of(p * rows, rows), rows)

    def blk(v, p, tt):
        return xg.at[v, rowpos(p), pl.ds(pl.multiple_of(tt * cols, cols), cols)]

    own = [pltpu.make_async_copy(acts.at[v], blk(v, pos, t), loc.at[v]) for v in range(2)]
    kload = pltpu.make_async_copy(types, kinds.at[pos], loc.at[2])
    gload = pltpu.make_async_copy(gains, gain_all.at[pos], loc.at[3])
    wload = [
        pltpu.make_async_copy(wq, wqv, loc.at[4]),
        pltpu.make_async_copy(wk, wkv, loc.at[5]),
        pltpu.make_async_copy(wv, wvv, loc.at[6]),
    ]
    hload = pltpu.make_async_copy(heads, hg, loc.at[7])
    grload = pltpu.make_async_copy(grads, gr, loc.at[8])
    for copy in own + [kload, gload] + wload + [hload, grload]:
        copy.start()

    barrier = pltpu.get_barrier_semaphore()
    greeted = [pos_peer(k) for k in range(1, SUB)] + [z_peer(k) for k in range(1, T)]
    greeted += [(before, t), (after, t)]
    for dev in greeted:
        pl.semaphore_signal(barrier, inc=1, device_id=dev, device_id_type=MESH)
    pl.semaphore_wait(barrier, len(greeted))

    def ag_send(kind, v, p, tt):
        dev = (left_dev, right_dev, x_dev, pair_dev)[kind]
        send(blk(v, p, tt), blk(v, p, tt), ag_s.at[v, kind, p, tt], ag_r.at[v, p, tt], dev)

    def ag_wait(v, p, tt):
        arrived(blk(v, p, tt), ag_r.at[v, p, tt])

    def ag_sides(v, p, tt):
        @pl.when(t > 0)
        def _():
            ag_send(LEFT, v, p, tt)

        @pl.when(t < T - 1)
        def _():
            ag_send(RIGHT, v, p, tt)

    own[0].wait()
    ag_send(ACROSS, 0, pos, t)
    own[1].wait()
    ag_sides(1, pos, t)
    ag_sides(0, pos, t)
    ag_send(ACROSS, 1, pos, t)
    ag_send(PAIR, 0, pos, t)
    ag_send(PAIR, 1, pos, t)
    kload.wait()
    gload.wait()
    for k in range(1, SUB):
        send(kinds.at[pos], kinds.at[pos], small_s.at[0, k], small_r.at[0, k], pos_peer(k))
        send(gain_all.at[pos], gain_all.at[pos], small_s.at[1, k], small_r.at[1, k], pos_peer(k))

    for copy in wload:
        copy.wait()

    def join_weights(v):
        for i in range(T):
            at = pl.ds(i * cols, cols)
            wcat[v, at, :hd] = wqv[v, at, :]
            kv_cols = jnp.concatenate([wkv[v, :, at], wvv[v, :, at]], axis=0)
            wcat[v, at, hd:] = jnp.transpose(kv_cols)

    acc[...] = jnp.zeros_like(acc)
    square[...] = jnp.zeros_like(square)

    def project(tt):
        for p in (pos_pair, (1 - xi) * 2 + (1 - ci)):
            for v in range(2):
                ag_wait(v, p, tt)
        block = tt * cols // gcols
        off = pl.multiple_of(lax.rem(tt * cols, gcols), cols)
        at = pl.ds(pl.multiple_of(tt * cols, cols), cols)
        for v in range(2):
            speech = kindc[v, :, 0:1] > 0.5
            pair = gain_all[block, v, :, pl.ds(off, cols)].astype(F32)
            xf = xg[v, :, at].astype(F32)
            square[v] += jnp.broadcast_to(jnp.sum(xf * xf, axis=1, keepdims=True), (n, 128))
            scaled = (xf * jnp.where(speech, pair[1:2, :], pair[0:1, :])).astype(BF16)
            acc[v] += dot(scaled, wcat[v, at, :], ((1,), (0,)))

    join_weights(0)

    ag_wait(0, pos_x, t)
    ag_sides(0, pos_x, t)
    ag_send(PAIR, 0, pos_x, t)

    def each_side(k, action):
        for low in (True, False):
            tt = t - k if low else t + k

            @pl.when(tt >= 0 if low else tt < T)
            def _():
                action(tt, low)

    def forward(tt, low):
        onward = t < T - 1 if low else t > 0
        kind = RIGHT if low else LEFT
        ag_wait(1, pos, tt)

        @pl.when(onward)
        def _():
            ag_send(kind, 1, pos, tt)

        ag_send(ACROSS, 1, pos, tt)
        ag_send(PAIR, 1, pos, tt)
        for p in (pos, pos_x):
            ag_wait(0, p, tt)

            @pl.when(onward)
            def _():
                ag_send(kind, 0, p, tt)

            ag_send(PAIR, 0, p, tt)

    def share(tt):
        ag_wait(1, pos_x, tt)
        ag_send(PAIR, 1, pos_x, tt)

    eye_r = lax.broadcasted_iota(jnp.int32, (rows, rows), 0) == lax.broadcasted_iota(
        jnp.int32, (rows, rows), 1
    )
    for k in range(1, T):
        each_side(k, forward)
        if k == 1:
            share(t)
            join_weights(1)
            for j in range(1, SUB):
                source = lax.rem(pos - j + SUB, SUB)
                arrived(kinds.at[source], small_r.at[0, j])
                arrived(gain_all.at[source], small_r.at[1, j])
            for v in range(2):
                for p in range(SUB):
                    line = kinds[p, v : v + 1, :].astype(F32)
                    column = jnp.sum(jnp.where(eye_r, line, 0.0), axis=1, keepdims=True)
                    kindc[v, p * rows : (p + 1) * rows, :] = jnp.broadcast_to(column, (rows, 128))
            project(t)
        else:
            each_side(k - 1, lambda tt, low: share(tt))
            each_side(k - 1, lambda tt, low: project(tt))
    each_side(T - 1, lambda tt, low: share(tt))
    each_side(T - 1, lambda tt, low: project(tt))

    hload.wait()
    eye = lax.broadcasted_iota(jnp.int32, (n, n), 0) == lax.broadcasted_iota(jnp.int32, (n, n), 1)
    mine = pl.ds(pl.multiple_of(t * kc, kc), kc)
    order = (1, 0)
    queries = [None, None]
    for v in order:
        inverse = lax.rsqrt(square[v][:, 0:1] / width + EPS)
        invc[v] = jnp.broadcast_to(inverse, (n, 128))
        projected = acc[v] * inverse
        turned = jnp.transpose(projected[:, hd:]).astype(BF16)
        kvt[v, 0, mine, :] = turned[:kc]
        kvt[v, 1, mine, :] = turned[kc:]
        for k in range(1, T):
            block = kvt.at[v, :, mine, :]
            send(block, block, kv_s.at[v, k], kv_r.at[v, k], z_peer(k))
        queries[v] = projected[:, :hd].astype(BF16)

    scale = hd ** (-0.5)
    causal = lax.broadcasted_iota(jnp.int32, (n, n), 0) >= lax.broadcasted_iota(
        jnp.int32, (n, n), 1
    )
    query_grads = [None, None]
    for v in order:
        for k in range(1, T):
            source = lax.rem(t - k + T, T)
            theirs = kvt.at[v, :, pl.ds(pl.multiple_of(source * kc, kc), kc), :]
            arrived(theirs, kv_r.at[v, k])
        kt = kvt[v, 0]
        vt = kvt[v, 1]
        og = hg[v]
        scores = dot(queries[v], kt, ((1,), (0,))) * scale
        scores = jnp.where(causal, scores, -1e30)
        top = jnp.max(scores, axis=1, keepdims=True)
        weights = jnp.exp(scores - top)
        probs = weights / jnp.sum(weights, axis=1, keepdims=True)
        pg = dot(og, vt, ((1,), (0,)))
        sg = probs * (pg - jnp.sum(pg * probs, axis=1, keepdims=True)) * scale
        sg = sg.astype(BF16)
        key_each = dot(queries[v], sg, ((0,), (0,)))
        value_each = dot(og, probs.astype(BF16), ((0,), (0,)))
        dkv[v, 0] = key_each.astype(BF16)
        dkv[v, 1] = value_each.astype(BF16)
        for k in range(1, T):
            goal = pl.ds(pl.multiple_of(lax.rem(t + k, T) * kc, kc), kc)
            send(dkv.at[v, :, goal, :], dkv_in.at[k - 1, v], dk_s.at[v, k], dk_r.at[v, k], z_peer(k))
        qg = dot(sg, kt, ((1,), (1,)))
        query_grads[v] = qg.astype(BF16)
        column = jnp.sum(qg * queries[v].astype(F32), axis=1, keepdims=True)
        line = jnp.sum(jnp.where(eye, column, 0.0), axis=0, keepdims=True)
        line = line + jnp.sum(
            key_each * kt.astype(F32) + value_each * vt.astype(F32), axis=0, keepdims=True
        )
        stat[v] = jnp.broadcast_to(line, (8, n))
    for k in range(1, T):
        send(stat, stat_z.at[k - 1], st_s.at[k], st_r.at[k], z_peer(k))

    goals = []
    for i in range((T + 1) // 2):
        goals += [T - 1 - i, i]
    goals = goals[:T]

    def terms(v, after_piece):
        summed = dkv[v, :, mine, :].astype(F32)
        for k in range(1, T):
            arrived(dkv_in.at[k - 1, v], dk_r.at[v, k])
            summed = summed + dkv_in[k - 1, v].astype(F32)
        kv_rows = jnp.transpose(summed.reshape(2 * kc, n)).astype(BF16)
        joined = jnp.concatenate([query_grads[v], kv_rows], axis=1)
        for j, i in enumerate(goals):
            piece = dot(joined, wcat[v, pl.ds(i * cols, cols), :], ((1,), (1,))).astype(BF16)
            for p in range(SUB):
                part[v, p // 2, p % 2, i] = piece[p * rows : (p + 1) * rows]
            send(part.at[v, :, 1 - ci, i], part_in.at[v, :, i], pair_s.at[v, i], pair_r.at[v, i], pair_dev)
            if j > 0:
                after_piece(goals[j - 1])
        after_piece(goals[-1])

    def held(v, i):
        return (
            part[v, xi, ci, i].astype(F32) + part_in[v, xi, i].astype(F32) + xr[v, i].astype(F32)
        )

    def pass_on(v, goal, right):
        side = 0 if right else 1
        dev = right_dev if right else left_dev
        send(zs.at[v, goal], zr.at[v, side, goal], z_s.at[v, goal], z_r.at[v, side, goal], dev)

    def begin(v, goal):
        arrived(xr.at[v, goal], x_r.at[v, goal])

        @pl.when(jnp.logical_and(t == 0, goal > 0))
        def _():
            zs[v, goal] = held(v, goal).astype(BF16)
            pass_on(v, goal, True)

        @pl.when(jnp.logical_and(t == T - 1, goal < T - 1))
        def _():
            zs[v, goal] = held(v, goal).astype(BF16)
            pass_on(v, goal, False)

    def relay(v, goal, right):
        side = 0 if right else 1
        arrived(zr.at[v, side, goal], z_r.at[v, side, goal])
        zs[v, goal] = (held(v, goal) + zr[v, side, goal].astype(F32)).astype(BF16)
        pass_on(v, goal, right)

    def cross(v, i):
        arrived(part_in.at[v, :, i], pair_r.at[v, i])
        xs[v, i] = (part[v, 1 - xi, ci, i].astype(F32) + part_in[v, 1 - xi, i].astype(F32)).astype(BF16)
        send(xs.at[v, i], xr.at[v, i], x_s.at[v, i], x_r.at[v, i], x_dev)

    def after_one(i):
        cross(1, i)

    def after_zero(i):
        cross(0, i)
        begin(1, i)

    terms(1, after_one)

    line = stat[...]
    for k in range(1, T):
        arrived(stat_z.at[k - 1], st_r.at[k])
        line = line + stat_z[k - 1]
    stat_s[...] = line
    for k in range(1, SUB):
        send(stat_s, stat_in.at[k - 1], sp_s.at[k], sp_r.at[k], pos_peer(k))

    terms(0, after_zero)

    def relays(v, i):
        high = T - 1 - i

        @pl.when(jnp.logical_and(t > 0, t < high))
        def _():
            relay(v, high, True)

        @pl.when(jnp.logical_and(t < T - 1, t > i))
        def _():
            relay(v, i, False)

    grload.wait()
    line = stat_s[...]
    for k in range(1, SUB):
        arrived(stat_in.at[k - 1], sp_r.at[k])
        line = line + stat_in[k - 1]
    lane = lax.broadcasted_iota(jnp.int32, (rows, n), 1)
    row = lax.broadcasted_iota(jnp.int32, (rows, n), 0)
    pick = lane == row + pos * rows
    gain_block = t * cols // gcols
    gain_off = pl.multiple_of(lax.rem(t * cols, gcols), cols)

    def finish(v):
        total[...] = held(v, t)
        for side in range(2):

            @pl.when(t > 0 if side == 0 else t < T - 1)
            def _():
                arrived(zr.at[v, side, t], z_r.at[v, side, t])
                total[...] += zr[v, side, t].astype(F32)

        mean = jnp.sum(jnp.where(pick, line[v, 0:1, :], 0.0), axis=1, keepdims=True) / width
        inverse = invc[v, rowpos(pos), 0:1]
        speech = kindc[v, rowpos(pos), 0:1] > 0.5
        pair = gain_all[gain_block, v, :, pl.ds(gain_off, cols)].astype(F32)
        gain = jnp.where(speech, pair[1:2, :], pair[0:1, :])
        x = xg[v, rowpos(pos), pl.ds(pl.multiple_of(t * cols, cols), cols)].astype(F32)
        res[v] = (
            gr[v].astype(F32) + inverse * gain * total[...] - x * (inverse * inverse * mean)
        ).astype(BF16)
        goal = jnp.where(here == 0, 1 - v, v)
        send(res.at[v], out.at[goal], route_s.at[v], route_r.at[goal], (before, t))

    for i in range(T - 1):
        relays(1, i)
    for i in goals:
        begin(0, i)
    relays(0, 0)
    finish(1)
    for i in range(1, T - 1):
        relays(0, i)
    finish(0)

    for v in range(2):
        for kind in (LEFT, RIGHT):
            edge = t > 0 if kind == LEFT else t < T - 1
            for tt in range(T):
                use = jnp.logical_and(edge, tt >= t if kind == LEFT else tt <= t)
                for p in (pos, pos_x):
                    if v == 1 and p is pos_x:
                        continue

                    @pl.when(use)
                    def _():
                        sent(blk(v, p, tt), ag_s.at[v, kind, p, tt])

        for tt in range(T):
            for p in (pos, pos_x):
                sent(blk(v, p, tt), ag_s.at[v, PAIR, p, tt])
            if v == 1:
                sent(blk(v, pos, tt), ag_s.at[v, ACROSS, pos, tt])
    sent(blk(0, pos, t), ag_s.at[0, ACROSS, pos, t])
    for k in range(1, SUB):
        sent(kinds.at[pos], small_s.at[0, k])
        sent(gain_all.at[pos], small_s.at[1, k])
        sent(stat_s, sp_s.at[k])
    for k in range(1, T):
        goal = pl.ds(pl.multiple_of(lax.rem(t + k, T) * kc, kc), kc)
        for v in range(2):
            sent(kvt.at[v, :, mine, :], kv_s.at[v, k])
            sent(dkv.at[v, :, goal, :], dk_s.at[v, k])
        sent(stat, st_s.at[k])
    for v in range(2):
        for i in range(T):
            sent(part.at[v, :, 1 - ci, i], pair_s.at[v, i])

            @pl.when(i != t)
            def _():
                sent(zs.at[v, i], z_s.at[v, i])
            sent(xs.at[v, i], x_s.at[v, i])
    for v in range(2):
        sent(res.at[v], route_s.at[v])
        arrived(out.at[v], route_r.at[v])


def per_device(sections, acts, grads_in, head_grads, types, gains, w_query, w_key, w_value):
    T = lax.axis_size("tensor")
    acts, grads_in, head_grads, types, gains = acts[0], grads_in[0], head_grads[0], types[0], gains[0]
    w_query, w_key, w_value = w_query[0], jnp.swapaxes(w_key[0], 1, 2), jnp.swapaxes(w_value[0], 1, 2)
    spans, rows, cols = acts.shape
    n = SUB * rows
    hd = w_query.shape[2]
    kc = w_key.shape[1]
    width = cols * T
    V = pltpu.VMEM
    D = pltpu.SemaphoreType.DMA
    scratch = [
        V((2, n, width), BF16), V((SUB, 2, rows), jnp.int32), V((SUB,) + gains.shape, BF16),
        V(w_query.shape, BF16), V(w_key.shape, BF16), V(w_value.shape, BF16),
        V((2, width, hd + 2 * kc), BF16), V(head_grads.shape, BF16), V(grads_in.shape, BF16),
        V((2, n, 128), F32), V((2, n, 128), F32), V((2, n, hd + 2 * kc), F32), V((2, n, 128), F32),
        V((2, 2, hd, n), BF16), V((2, 2, hd, n), BF16), V((T - 1, 2, 2, kc, n), BF16),
        V((2, 8, n), F32), V((T - 1, 2, 8, n), F32), V((2, 8, n), F32), V((SUB - 1, 2, 8, n), F32),
        V((2, 2, 2, T, rows, cols), BF16), V((2, 2, T, rows, cols), BF16),
        V((2, T, rows, cols), BF16), V((2, T, rows, cols), BF16),
        V((2, T, rows, cols), BF16), V((2, 2, T, rows, cols), BF16),
        V((rows, cols), F32), V((2, rows, cols), BF16),
        D((9,)), D((2, 4, SUB, T)), D((2, SUB, T)), D((2, SUB)), D((2, SUB)),
        D((2, T)), D((2, T)), D((2, T)), D((2, T)), D((T,)), D((T,)), D((SUB,)), D((SUB,)),
        D((2, T)), D((2, T)), D((2, T)), D((2, T)), D((2, T)), D((2, 2, T)), D((2,)), D((2,)),
    ]

    def body(*refs):
        kernel(sections, T, *refs)

    routed = pl.pallas_call(
        body,
        out_shape=jax.ShapeDtypeStruct((2, rows, cols), BF16),
        in_specs=[pl.BlockSpec(memory_space=pl.ANY)] * 8,
        out_specs=pl.BlockSpec(memory_space=pltpu.VMEM),
        scratch_shapes=scratch,
        compiler_params=pltpu.CompilerParams(
            collective_id=0, has_side_effects=True, vmem_limit_bytes=50 * 1024 * 1024
        ),
        name="relay",
    )(acts, grads_in, head_grads, types, gains, w_query, w_key, w_value)
    return routed[None]


def solution(mesh):
    sections = mesh.shape["section"] // SUB

    def run(*args):
        return per_device(sections, *args)

    return jax.shard_map(
        run,
        mesh=mesh,
        in_specs=(
            P("section", None, None, "tensor"),
            P("section", None, None, "tensor"),
            P("section", None, None, "tensor"),
            P("section", None, None),
            P("section", None, None, None),
            P("section", None, None, "tensor"),
            P("section", None, None, "tensor"),
            P("section", None, None, "tensor"),
        ),
        out_specs=P("section", None, None, "tensor"),
        check_vma=False,
    )
```

```python
import jax
import jax.numpy as jnp
from jax import lax
from jax.experimental import pallas as pl
from jax.experimental.pallas import tpu as pltpu
from jax.sharding import PartitionSpec as P

SUB = 4
EPS = 1e-05
MESH = pl.DeviceIdType.MESH
F32 = jnp.float32
BF16 = jnp.bfloat16
LEFT, RIGHT, ACROSS, PAIR = 0, 1, 2, 3


def dot(a, b, dims):
    return lax.dot_general(a, b, (dims, ((), ())), preferred_element_type=F32)


def kernel(
    sections, tensors,
    acts, grads, heads, types, gains, wq, wk, wv,
    out,
    xg, kinds, gain_all, wqv, wkv, wvv, wcat, hg, gr, kindc, invc, acc, square,
    kvt, dkv, dkv_in, stat, stat_z, stat_s, stat_in,
    part, part_in, xs, xr, zs, zr, total, res,
    loc, ag_s, ag_r, small_s, small_r, kv_s, kv_r, dk_s, dk_r, st_s, st_r, sp_s, sp_r,
    pair_s, pair_r, x_s, x_r, z_s, z_r, route_s, route_r,
):
    spans, rows, cols = acts.shape
    n = SUB * rows
    hd = wq.shape[2]
    kc = wk.shape[1]
    width = cols * tensors
    gcols = gains.shape[2]
    T = tensors
    t = lax.axis_index("tensor")
    sec = lax.axis_index("section")
    pos = lax.rem(sec, SUB)
    here = sec // SUB
    base = here * SUB
    xi = pos // 2
    ci = lax.rem(pos, 2)
    pos_pair = xi * 2 + (1 - ci)
    pos_x = (1 - xi) * 2 + ci
    pair_dev = (base + pos_pair, t)
    x_dev = (base + pos_x, t)
    left_dev = (sec, lax.max(t - 1, 0))
    right_dev = (sec, lax.min(t + 1, T - 1))
    before = lax.rem(here + sections - 1, sections) * SUB + pos
    after = lax.rem(here + 1, sections) * SUB + pos

    def pos_peer(k):
        return (base + lax.rem(pos + k, SUB), t)

    def z_peer(k):
        return (sec, lax.rem(t + k, T))

    def send(src, dst, ssem, rsem, dev):
        pltpu.make_async_remote_copy(
            src_ref=src, dst_ref=dst, send_sem=ssem, recv_sem=rsem, device_id=dev, device_id_type=MESH
        ).start()

    def sent(src, ssem):
        pltpu.make_async_copy(src, src, ssem).wait()

    def arrived(dst, rsem):
        pltpu.make_async_copy(dst, dst, rsem).wait()

    def rowpos(p):
        return pl.ds(pl.multiple_of(p * rows, rows), rows)

    def blk(v, p, tt):
        return xg.at[v, rowpos(p), pl.ds(pl.multiple_of(tt * cols, cols), cols)]

    own = [pltpu.make_async_copy(acts.at[v], blk(v, pos, t), loc.at[v]) for v in range(2)]
    kload = pltpu.make_async_copy(types, kinds.at[pos], loc.at[2])
    gload = pltpu.make_async_copy(gains, gain_all.at[pos], loc.at[3])
    wload = [
        pltpu.make_async_copy(wq, wqv, loc.at[4]),
        pltpu.make_async_copy(wk, wkv, loc.at[5]),
        pltpu.make_async_copy(wv, wvv, loc.at[6]),
    ]
    hload = pltpu.make_async_copy(heads, hg, loc.at[7])
    grload = pltpu.make_async_copy(grads, gr, loc.at[8])
    for copy in own + [kload, gload] + wload + [hload, grload]:
        copy.start()

    barrier = pltpu.get_barrier_semaphore()
    greeted = [pos_peer(k) for k in range(1, SUB)] + [z_peer(k) for k in range(1, T)]
    greeted += [(before, t), (after, t)]
    for dev in greeted:
        pl.semaphore_signal(barrier, inc=1, device_id=dev, device_id_type=MESH)
    pl.semaphore_wait(barrier, len(greeted))

    def ag_send(kind, v, p, tt):
        dev = (left_dev, right_dev, x_dev, pair_dev)[kind]
        send(blk(v, p, tt), blk(v, p, tt), ag_s.at[v, kind, p, tt], ag_r.at[v, p, tt], dev)

    def ag_wait(v, p, tt):
        arrived(blk(v, p, tt), ag_r.at[v, p, tt])

    def ag_sides(v, p, tt):
        @pl.when(t > 0)
        def _():
            ag_send(LEFT, v, p, tt)

        @pl.when(t < T - 1)
        def _():
            ag_send(RIGHT, v, p, tt)

    own[0].wait()
    ag_send(ACROSS, 0, pos, t)
    own[1].wait()
    ag_sides(1, pos, t)
    ag_sides(0, pos, t)
    ag_send(ACROSS, 1, pos, t)
    ag_send(PAIR, 0, pos, t)
    ag_send(PAIR, 1, pos, t)
    kload.wait()
    gload.wait()
    for k in range(1, SUB):
        send(kinds.at[pos], kinds.at[pos], small_s.at[0, k], small_r.at[0, k], pos_peer(k))
        send(gain_all.at[pos], gain_all.at[pos], small_s.at[1, k], small_r.at[1, k], pos_peer(k))

    for copy in wload:
        copy.wait()

    def join_weights(v):
        for i in range(T):
            at = pl.ds(i * cols, cols)
            wcat[v, at, :hd] = wqv[v, at, :]
            kv_cols = jnp.concatenate([wkv[v, :, at], wvv[v, :, at]], axis=0)
            wcat[v, at, hd:] = jnp.transpose(kv_cols)

    acc[...] = jnp.zeros_like(acc)
    square[...] = jnp.zeros_like(square)

    def project(tt):
        for p in (pos_pair, (1 - xi) * 2 + (1 - ci)):
            for v in range(2):
                ag_wait(v, p, tt)
        block = tt * cols // gcols
        off = pl.multiple_of(lax.rem(tt * cols, gcols), cols)
        at = pl.ds(pl.multiple_of(tt * cols, cols), cols)
        for v in range(2):
            speech = kindc[v, :, 0:1] > 0.5
            pair = gain_all[block, v, :, pl.ds(off, cols)].astype(F32)
            xf = xg[v, :, at].astype(F32)
            square[v] += jnp.broadcast_to(jnp.sum(xf * xf, axis=1, keepdims=True), (n, 128))
            scaled = (xf * jnp.where(speech, pair[1:2, :], pair[0:1, :])).astype(BF16)
            acc[v] += dot(scaled, wcat[v, at, :], ((1,), (0,)))

    join_weights(0)

    ag_wait(0, pos_x, t)
    ag_sides(0, pos_x, t)
    ag_send(PAIR, 0, pos_x, t)

    def each_side(k, action):
        for low in (True, False):
            tt = t - k if low else t + k

            @pl.when(tt >= 0 if low else tt < T)
            def _():
                action(tt, low)

    def forward(tt, low):
        onward = t < T - 1 if low else t > 0
        kind = RIGHT if low else LEFT
        ag_wait(1, pos, tt)

        @pl.when(onward)
        def _():
            ag_send(kind, 1, pos, tt)

        ag_send(ACROSS, 1, pos, tt)
        ag_send(PAIR, 1, pos, tt)
        for p in (pos, pos_x):
            ag_wait(0, p, tt)

            @pl.when(onward)
            def _():
                ag_send(kind, 0, p, tt)

            ag_send(PAIR, 0, p, tt)

    def share(tt):
        ag_wait(1, pos_x, tt)
        ag_send(PAIR, 1, pos_x, tt)

    eye_r = lax.broadcasted_iota(jnp.int32, (rows, rows), 0) == lax.broadcasted_iota(
        jnp.int32, (rows, rows), 1
    )
    for k in range(1, T):
        each_side(k, forward)
        if k == 1:
            share(t)
            join_weights(1)
            for j in range(1, SUB):
                source = lax.rem(pos - j + SUB, SUB)
                arrived(kinds.at[source], small_r.at[0, j])
                arrived(gain_all.at[source], small_r.at[1, j])
            for v in range(2):
                for p in range(SUB):
                    line = kinds[p, v : v + 1, :].astype(F32)
                    column = jnp.sum(jnp.where(eye_r, line, 0.0), axis=1, keepdims=True)
                    kindc[v, p * rows : (p + 1) * rows, :] = jnp.broadcast_to(column, (rows, 128))
            project(t)
        else:
            each_side(k - 1, lambda tt, low: share(tt))
            each_side(k - 1, lambda tt, low: project(tt))
    each_side(T - 1, lambda tt, low: share(tt))
    each_side(T - 1, lambda tt, low: project(tt))

    hload.wait()
    eye = lax.broadcasted_iota(jnp.int32, (n, n), 0) == lax.broadcasted_iota(jnp.int32, (n, n), 1)
    mine = pl.ds(pl.multiple_of(t * kc, kc), kc)
    order = (1, 0)
    queries = [None, None]
    for v in order:
        inverse = lax.rsqrt(square[v][:, 0:1] / width + EPS)
        invc[v] = jnp.broadcast_to(inverse, (n, 128))
        projected = acc[v] * inverse
        turned = jnp.transpose(projected[:, hd:]).astype(BF16)
        kvt[v, 0, mine, :] = turned[:kc]
        kvt[v, 1, mine, :] = turned[kc:]
        for k in range(1, T):
            block = kvt.at[v, :, mine, :]
            send(block, block, kv_s.at[v, k], kv_r.at[v, k], z_peer(k))
        queries[v] = projected[:, :hd].astype(BF16)

    scale = hd ** (-0.5)
    causal = lax.broadcasted_iota(jnp.int32, (n, n), 0) >= lax.broadcasted_iota(
        jnp.int32, (n, n), 1
    )
    query_grads = [None, None]
    for v in order:
        for k in range(1, T):
            source = lax.rem(t - k + T, T)
            theirs = kvt.at[v, :, pl.ds(pl.multiple_of(source * kc, kc), kc), :]
            arrived(theirs, kv_r.at[v, k])
        kt = kvt[v, 0]
        vt = kvt[v, 1]
        og = hg[v]
        scores = dot(queries[v], kt, ((1,), (0,))) * scale
        scores = jnp.where(causal, scores, -1e30)
        top = jnp.max(scores, axis=1, keepdims=True)
        weights = jnp.exp(scores - top)
        probs = weights / jnp.sum(weights, axis=1, keepdims=True)
        pg = dot(og, vt, ((1,), (0,)))
        sg = probs * (pg - jnp.sum(pg * probs, axis=1, keepdims=True)) * scale
        sg = sg.astype(BF16)
        key_each = dot(queries[v], sg, ((0,), (0,)))
        value_each = dot(og, probs.astype(BF16), ((0,), (0,)))
        dkv[v, 0] = key_each.astype(BF16)
        dkv[v, 1] = value_each.astype(BF16)
        for k in range(1, T):
            goal = pl.ds(pl.multiple_of(lax.rem(t + k, T) * kc, kc), kc)
            send(dkv.at[v, :, goal, :], dkv_in.at[k - 1, v], dk_s.at[v, k], dk_r.at[v, k], z_peer(k))
        qg = dot(sg, kt, ((1,), (1,)))
        query_grads[v] = qg.astype(BF16)
        column = jnp.sum(qg * queries[v].astype(F32), axis=1, keepdims=True)
        line = jnp.sum(jnp.where(eye, column, 0.0), axis=0, keepdims=True)
        line = line + jnp.sum(
            key_each * kt.astype(F32) + value_each * vt.astype(F32), axis=0, keepdims=True
        )
        stat[v] = jnp.broadcast_to(line, (8, n))
    for k in range(1, T):
        send(stat, stat_z.at[k - 1], st_s.at[k], st_r.at[k], z_peer(k))

    goals = []
    for i in range((T + 1) // 2):
        goals += [T - 1 - i, i]
    goals = goals[:T]

    def terms(v, after_piece):
        summed = dkv[v, :, mine, :].astype(F32)
        for k in range(1, T):
            arrived(dkv_in.at[k - 1, v], dk_r.at[v, k])
            summed = summed + dkv_in[k - 1, v].astype(F32)
        kv_rows = jnp.transpose(summed.reshape(2 * kc, n)).astype(BF16)
        joined = jnp.concatenate([query_grads[v], kv_rows], axis=1)
        for j, i in enumerate(goals):
            piece = dot(joined, wcat[v, pl.ds(i * cols, cols), :], ((1,), (1,))).astype(BF16)
            for p in range(SUB):
                part[v, p // 2, p % 2, i] = piece[p * rows : (p + 1) * rows]
            send(part.at[v, :, 1 - ci, i], part_in.at[v, :, i], pair_s.at[v, i], pair_r.at[v, i], pair_dev)
            if j > 0:
                after_piece(goals[j - 1])
        after_piece(goals[-1])

    def held(v, i):
        return (
            part[v, xi, ci, i].astype(F32) + part_in[v, xi, i].astype(F32) + xr[v, i].astype(F32)
        )

    def pass_on(v, goal, right):
        side = 0 if right else 1
        dev = right_dev if right else left_dev
        send(zs.at[v, goal], zr.at[v, side, goal], z_s.at[v, goal], z_r.at[v, side, goal], dev)

    def begin(v, goal):
        arrived(xr.at[v, goal], x_r.at[v, goal])

        @pl.when(jnp.logical_and(t == 0, goal > 0))
        def _():
            zs[v, goal] = held(v, goal).astype(BF16)
            pass_on(v, goal, True)

        @pl.when(jnp.logical_and(t == T - 1, goal < T - 1))
        def _():
            zs[v, goal] = held(v, goal).astype(BF16)
            pass_on(v, goal, False)

    def relay(v, goal, right):
        side = 0 if right else 1
        arrived(zr.at[v, side, goal], z_r.at[v, side, goal])
        zs[v, goal] = (held(v, goal) + zr[v, side, goal].astype(F32)).astype(BF16)
        pass_on(v, goal, right)

    def cross(v, i):
        arrived(part_in.at[v, :, i], pair_r.at[v, i])
        xs[v, i] = (part[v, 1 - xi, ci, i].astype(F32) + part_in[v, 1 - xi, i].astype(F32)).astype(BF16)
        send(xs.at[v, i], xr.at[v, i], x_s.at[v, i], x_r.at[v, i], x_dev)

    def after_one(i):
        cross(1, i)

    def after_zero(i):
        cross(0, i)
        begin(1, i)

    terms(1, after_one)

    line = stat[...]
    for k in range(1, T):
        arrived(stat_z.at[k - 1], st_r.at[k])
        line = line + stat_z[k - 1]
    stat_s[...] = line
    for k in range(1, SUB):
        send(stat_s, stat_in.at[k - 1], sp_s.at[k], sp_r.at[k], pos_peer(k))

    terms(0, after_zero)

    def relays(v, i):
        high = T - 1 - i

        @pl.when(jnp.logical_and(t > 0, t < high))
        def _():
            relay(v, high, True)

        @pl.when(jnp.logical_and(t < T - 1, t > i))
        def _():
            relay(v, i, False)

    grload.wait()
    line = stat_s[...]
    for k in range(1, SUB):
        arrived(stat_in.at[k - 1], sp_r.at[k])
        line = line + stat_in[k - 1]
    lane = lax.broadcasted_iota(jnp.int32, (rows, n), 1)
    row = lax.broadcasted_iota(jnp.int32, (rows, n), 0)
    pick = lane == row + pos * rows
    gain_block = t * cols // gcols
    gain_off = pl.multiple_of(lax.rem(t * cols, gcols), cols)

    def finish(v):
        total[...] = held(v, t)
        for side in range(2):

            @pl.when(t > 0 if side == 0 else t < T - 1)
            def _():
                arrived(zr.at[v, side, t], z_r.at[v, side, t])
                total[...] += zr[v, side, t].astype(F32)

        mean = jnp.sum(jnp.where(pick, line[v, 0:1, :], 0.0), axis=1, keepdims=True) / width
        inverse = invc[v, rowpos(pos), 0:1]
        speech = kindc[v, rowpos(pos), 0:1] > 0.5
        pair = gain_all[gain_block, v, :, pl.ds(gain_off, cols)].astype(F32)
        gain = jnp.where(speech, pair[1:2, :], pair[0:1, :])
        x = xg[v, rowpos(pos), pl.ds(pl.multiple_of(t * cols, cols), cols)].astype(F32)
        res[v] = (
            gr[v].astype(F32) + inverse * gain * total[...] - x * (inverse * inverse * mean)
        ).astype(BF16)
        goal = jnp.where(here == 0, 1 - v, v)
        send(res.at[v], out.at[goal], route_s.at[v], route_r.at[goal], (before, t))

    for i in range(T - 1):
        relays(1, i)
    for i in goals:
        begin(0, i)
    relays(0, 0)
    finish(1)
    for i in range(1, T - 1):
        relays(0, i)
    finish(0)

    for v in range(2):
        for kind in (LEFT, RIGHT):
            edge = t > 0 if kind == LEFT else t < T - 1
            for tt in range(T):
                use = jnp.logical_and(edge, tt >= t if kind == LEFT else tt <= t)
                for p in (pos, pos_x):
                    if v == 1 and p is pos_x:
                        continue

                    @pl.when(use)
                    def _():
                        sent(blk(v, p, tt), ag_s.at[v, kind, p, tt])

        for tt in range(T):
            for p in (pos, pos_x):
                sent(blk(v, p, tt), ag_s.at[v, PAIR, p, tt])
            if v == 1:
                sent(blk(v, pos, tt), ag_s.at[v, ACROSS, pos, tt])
    sent(blk(0, pos, t), ag_s.at[0, ACROSS, pos, t])
    for k in range(1, SUB):
        sent(kinds.at[pos], small_s.at[0, k])
        sent(gain_all.at[pos], small_s.at[1, k])
        sent(stat_s, sp_s.at[k])
    for k in range(1, T):
        goal = pl.ds(pl.multiple_of(lax.rem(t + k, T) * kc, kc), kc)
        for v in range(2):
            sent(kvt.at[v, :, mine, :], kv_s.at[v, k])
            sent(dkv.at[v, :, goal, :], dk_s.at[v, k])
        sent(stat, st_s.at[k])
    for v in range(2):
        for i in range(T):
            sent(part.at[v, :, 1 - ci, i], pair_s.at[v, i])

            @pl.when(i != t)
            def _():
                sent(zs.at[v, i], z_s.at[v, i])
            sent(xs.at[v, i], x_s.at[v, i])
    for v in range(2):
        sent(res.at[v], route_s.at[v])
        arrived(out.at[v], route_r.at[v])


def per_device(sections, acts, grads_in, head_grads, types, gains, w_query, w_key, w_value):
    T = lax.axis_size("tensor")
    acts, grads_in, head_grads, types, gains = acts[0], grads_in[0], head_grads[0], types[0], gains[0]
    w_query, w_key, w_value = w_query[0], jnp.swapaxes(w_key[0], 1, 2), jnp.swapaxes(w_value[0], 1, 2)
    spans, rows, cols = acts.shape
    n = SUB * rows
    hd = w_query.shape[2]
    kc = w_key.shape[1]
    width = cols * T
    V = pltpu.VMEM
    D = pltpu.SemaphoreType.DMA
    scratch = [
        V((2, n, width), BF16), V((SUB, 2, rows), jnp.int32), V((SUB,) + gains.shape, BF16),
        V(w_query.shape, BF16), V(w_key.shape, BF16), V(w_value.shape, BF16),
        V((2, width, hd + 2 * kc), BF16), V(head_grads.shape, BF16), V(grads_in.shape, BF16),
        V((2, n, 128), F32), V((2, n, 128), F32), V((2, n, hd + 2 * kc), F32), V((2, n, 128), F32),
        V((2, 2, hd, n), BF16), V((2, 2, hd, n), BF16), V((T - 1, 2, 2, kc, n), BF16),
        V((2, 8, n), F32), V((T - 1, 2, 8, n), F32), V((2, 8, n), F32), V((SUB - 1, 2, 8, n), F32),
        V((2, 2, 2, T, rows, cols), BF16), V((2, 2, T, rows, cols), BF16),
        V((2, T, rows, cols), BF16), V((2, T, rows, cols), BF16),
        V((2, T, rows, cols), BF16), V((2, 2, T, rows, cols), BF16),
        V((rows, cols), F32), V((2, rows, cols), BF16),
        D((9,)), D((2, 4, SUB, T)), D((2, SUB, T)), D((2, SUB)), D((2, SUB)),
        D((2, T)), D((2, T)), D((2, T)), D((2, T)), D((T,)), D((T,)), D((SUB,)), D((SUB,)),
        D((2, T)), D((2, T)), D((2, T)), D((2, T)), D((2, T)), D((2, 2, T)), D((2,)), D((2,)),
    ]

    def body(*refs):
        kernel(sections, T, *refs)

    routed = pl.pallas_call(
        body,
        out_shape=jax.ShapeDtypeStruct((2, rows, cols), BF16),
        in_specs=[pl.BlockSpec(memory_space=pl.ANY)] * 8,
        out_specs=pl.BlockSpec(memory_space=pltpu.VMEM),
        scratch_shapes=scratch,
        compiler_params=pltpu.CompilerParams(
            collective_id=0, has_side_effects=True, vmem_limit_bytes=67_000_000
        ),
        name="relay",
    )(acts, grads_in, head_grads, types, gains, w_query, w_key, w_value)
    return routed[None]


def solution(mesh):
    sections = mesh.shape["section"] // SUB

    def run(*args):
        return per_device(sections, *args)

    return jax.shard_map(
        run,
        mesh=mesh,
        in_specs=(
            P("section", None, None, "tensor"),
            P("section", None, None, "tensor"),
            P("section", None, None, "tensor"),
            P("section", None, None),
            P("section", None, None, None),
            P("section", None, None, "tensor"),
            P("section", None, None, "tensor"),
            P("section", None, None, "tensor"),
        ),
        out_specs=P("section", None, None, "tensor"),
        check_vma=False,
    )
```
